32 devices in a mesh: img: 2 (over y), sub: 4 (over z), rng: 4 (over x, core).
Axes of the slice: x: 2, y: 2, z: 4, core: 2. Of those that a mesh axis runs over, the one named last changes fastest.
Arguments:
- image: bfloat16 [2, 16, 128, 4096], P(None, ('img', 'sub'), None, 'rng'), parts along dimension 1, may hold values from -6 to 6
- interp_weights: bfloat16 [4, 2, 2, 2, 128, 128], replicated, may hold values from -0.25 to 0.25
- range_taps: float32 [4, 4], replicated, may hold values from -2 to 2
- range_shifts: int32 [4, 2, 128], replicated, may hold values from -8 to 5
Outputs:
- merged_image: bfloat16 [2, 16, 128, 4096], P(None, ('img', 'sub'), None, 'rng'), parts along dimension 1
The draws below stay inside these ranges and needn't reach their ends.
There are 2 independent parts, one for each index of `img`. The reference program is written for one: setup_inputs(seed, part) draws one part's arguments, and reference() takes and returns one part's arrays. A program takes and returns all parts, laid end to end along the dimension named above; an argument that names none is the same for every part. Nothing has to cross between parts.
All inputs are finite; a program needn't handle non-finite values.
Results may differ from the reference program's by a relative error of at most 0.0095.
Values may be sent and summed in bfloat16 or wider, within the bound.
No kernel may reach another device: no remote copies, remote signals or barrier semaphores. Data moves between devices by JAX's collectives and lax.ppermute only.
A program may use at most 64 MiB of HBM per device.

```python
import math
import jax
import jax.numpy as jnp
import numpy as np

ANGLES = 128
RANGE = 4096
RIM = 8
TAPS = 4
LEVELS = 4
GROUPS = 2
SUBIMAGES = 8
N_SUB = 4


def touch_ends(entries, rng, smallest, top_value):
    spot = [jax.random.randint(jax.random.fold_in(rng, axis), (), 0, length) for axis, length in enumerate(entries.shape)]
    widest = entries.shape.index(max(entries.shape))
    next_to = spot[:widest] + [(spot[widest] + 1) % entries.shape[widest]] + spot[widest + 1:]
    return entries.at[tuple(spot)].set(smallest).at[tuple(next_to)].set(top_value)


def block_levels(own_key, dims, cuts, least, high):
    gain, own = 1.0, jax.random.fold_in(own_key, 6)
    for dim, shards_of in cuts:
        draws = jnp.exp(jax.random.uniform(jax.random.fold_in(own, dim), (shards_of,), jnp.float32, least / len(cuts), high / len(cuts)))
        gain = gain * jnp.repeat(draws, dims[dim] // shards_of).reshape([-1 if axis == dim else 1 for axis in range(len(dims))])
    return gain


def normal_values(stream_key, shape, deviation, bound, cuts=(), held_as=jnp.bfloat16):
    entries = deviation * jax.random.normal(stream_key, shape, jnp.float32)
    if cuts:
        entries = entries * block_levels(stream_key, shape, cuts, -0.22, 0.18)
    return jnp.clip(entries, -bound, bound).astype(held_as)


def setup_inputs(seed: int = 0, part: int = 0) -> dict:
    streams_of = jax.random.split(jax.random.key(seed), 5)
    part_keys = jax.random.split(jax.random.fold_in(streams_of[4], part), 5)
    image = normal_values(part_keys[0], (2, SUBIMAGES, ANGLES, RANGE), 1.0, 6.0, ((1, 4), (3, 4)))
    interp_weights = normal_values(streams_of[1], (LEVELS, 2, 2, 2, ANGLES, ANGLES), (4 * ANGLES) ** -0.5, 0.25)
    range_taps = normal_values(streams_of[2], (LEVELS, TAPS), 0.5, 2.0, (), jnp.float32)
    range_shifts = touch_ends(jax.random.randint(streams_of[3], (LEVELS, 2, ANGLES), 0 - RIM, RIM - TAPS + 2), jax.random.fold_in(streams_of[3], 1), 0 - RIM, (RIM - TAPS + 2) - 1).astype(jnp.int32)
    return dict(image=image, interp_weights=interp_weights, range_taps=range_taps, range_shifts=range_shifts)


phase_step = 2.0 * math.pi / 64.0


def rotate(merged_sum, level_index, half_index, range_start, range_width):
    angle_rows = half_index * ANGLES + jnp.arange(ANGLES, dtype=jnp.int32)
    range_cols = range_start + jnp.arange(range_width, dtype=jnp.int32)
    wrapped = (range_cols[None, :] * (angle_rows[:, None] + 1) * (7 + level_index)) % 64
    phase = wrapped.astype(jnp.float32) * phase_step
    cosine = jnp.cos(phase)
    sinus = jnp.sin(phase)
    return jnp.stack([merged_sum[0] * cosine - merged_sum[1] * sinus, merged_sum[0] * sinus + merged_sum[1] * cosine])


def reference(image, interp_weights, range_taps, range_shifts):
    bit_count = N_SUB.bit_length() - 1
    count = N_SUB * GROUPS
    current = image
    for level_index in range(LEVELS):
        bit = level_index % bit_count
        stride = 2 ** bit
        side_of_rows = (np.arange(count) // GROUPS // stride) % 2
        padded = jnp.pad(current, ((0, 0), (0, 0), (0, 0), (RIM, RIM)))
        shift_rows = range_shifts[level_index][side_of_rows]
        base_index = (RIM + shift_rows[:, :, None] + jnp.arange(RANGE, dtype=jnp.int32)[None, None, :]).astype(jnp.int32)
        total = jnp.zeros(current.shape, jnp.float32)
        for tap_index in range(TAPS):
            gathered = jnp.stack([jnp.take_along_axis(padded[channel], base_index + tap_index, axis=2) for channel in range(2)])
            total = total + range_taps[level_index, tap_index] * gathered.astype(jnp.float32)
        interpolated = total.astype(jnp.bfloat16)
        split_rows = interpolated.reshape(2, N_SUB // (2 * stride), 2, stride, GROUPS, ANGLES, RANGE)
        half_images = []
        for half_index in range(2):
            merged_sum = jnp.zeros((2, N_SUB // (2 * stride), stride, GROUPS, ANGLES, RANGE), jnp.float32)
            for side_index in range(2):
                weight_pair = interp_weights[level_index, side_index, half_index].astype(jnp.float32)
                block_matrix = jnp.stack([jnp.stack([weight_pair[0], -weight_pair[1]]), jnp.stack([weight_pair[1], weight_pair[0]])])
                source = split_rows[:, :, side_index].astype(jnp.float32)
                merged_sum = merged_sum + jnp.einsum('xcij,chmgjr->xhmgir', block_matrix, source)
            half_images.append(rotate(merged_sum, level_index, half_index, 0, RANGE))
        current = jnp.stack(half_images, axis=2).reshape(2, count, ANGLES, RANGE).astype(jnp.bfloat16)
    return current
```

```python
import functools
import math

import jax
import jax.numpy as jnp
import numpy as np
from jax import lax
from jax.experimental import pallas as pl
from jax.experimental.pallas import tpu as pltpu
from jax.sharding import PartitionSpec as P

ANGLES = 128
RIM = 8
TAPS = 4
LEVELS = 4
LANES = 128
PERIOD = 64
ROWS = 32


def phases_of(bit_count):
    runs = []
    for level in range(LEVELS):
        bit = level % bit_count
        if runs and len(set(runs[-1][1] + [bit])) <= 2:
            runs[-1][0].append(level)
            runs[-1][1].append(bit)
        else:
            runs.append(([level], [bit]))
    return [(levels, bits, sorted(set(bits))) for levels, bits in runs]


def phase_table(levels, margin):
    cols = np.arange(LANES, dtype=np.int64) - margin
    rows = np.arange(2 * ANGLES, dtype=np.int64) + 1
    out = []
    for level in levels:
        wrapped = (cols[None, :] * rows[:, None] * (7 + level)) % PERIOD
        phase = wrapped.astype(np.float64) * (2.0 * math.pi / PERIOD)
        out.append(np.stack([np.cos(phase), np.sin(phase)]).reshape(2, 2, ANGLES, LANES))
    return np.stack(out).astype(np.float32)


def shift_masks(range_shifts):
    steps = range_shifts + RIM
    bits = [(steps >> k) & 1 for k in range(3)] + [1 - ((steps >> 3) & 1)]
    return jnp.stack(bits, axis=-1)


def merge_kernel(start_ref, taps_ref, masks_ref, weights_ref, table_ref, in_ref, out_ref,
                 x_ref, y_ref, w_ref, *, places, margin, total):
    members, _, wide = x_ref.shape
    given = in_ref.shape[-1]
    width = out_ref.shape[-1]
    start = start_ref[0]
    n_levels = len(places)
    x_ref[:, :, wide - LANES:] = jnp.zeros((members, 2 * ANGLES, LANES), jnp.bfloat16)
    x_ref[:, :, 0:given] = in_ref[...]
    for level in range(n_levels):
        place = places[level]
        for h in range(2):
            for e in range(2):
                real = weights_ref[level, e, h, 0]
                imag = weights_ref[level, e, h, 1]
                r0, c0 = h * 2 * ANGLES, e * 2 * ANGLES
                w_ref[r0:r0 + ANGLES, c0:c0 + ANGLES] = real
                w_ref[r0:r0 + ANGLES, c0 + ANGLES:c0 + 2 * ANGLES] = -imag
                w_ref[r0 + ANGLES:r0 + 2 * ANGLES, c0:c0 + ANGLES] = imag
                w_ref[r0 + ANGLES:r0 + 2 * ANGLES, c0 + ANGLES:c0 + 2 * ANGLES] = real
        taps = [taps_ref[level, t] for t in range(TAPS)]

        for side in range(2):
            own = [p for p in range(members) if (p >> place) % 2 == side]

            def rows_step(block, carry, side=side, own=own, level=level, taps=taps):
                flags = masks_ref[level, side, pl.ds(pl.multiple_of(block * ROWS, ROWS), ROWS), :]
                masks = [jnp.broadcast_to(flags[:, k:k + 1], (ROWS, wide)) != 0 for k in range(4)]
                for p in own:
                    for c in range(2):
                        rows = pl.ds(pl.multiple_of(c * ANGLES + block * ROWS, ROWS), ROWS)
                        cells = x_ref[p, rows, :].astype(jnp.float32)
                        after = pltpu.roll(cells, wide - 1, 1)
                        first = taps[0] * cells + taps[1] * after
                        second = taps[2] * cells + taps[3] * after
                        v = first + pltpu.roll(second, wide - 2, 1)
                        for k, by in ((0, wide - 1), (1, wide - 2), (2, wide - 4), (3, RIM)):
                            v = jnp.where(masks[k], pltpu.roll(v, by, 1), v)
                        y_ref[p, rows, :] = v.astype(jnp.bfloat16)
                return carry

            lax.fori_loop(0, ANGLES // ROWS, rows_step, 0)

        last = level == n_levels - 1
        cols = start + lax.broadcasted_iota(jnp.int32, (ANGLES, LANES), 1)
        for low in [p for p in range(members) if (p >> place) % 2 == 0]:
            high = low + 2 ** place
            for h in range(2):
                r0 = h * 2 * ANGLES
                z = jnp.dot(w_ref[r0:r0 + 2 * ANGLES, 0:2 * ANGLES], y_ref[low], preferred_element_type=jnp.float32)
                z = z + jnp.dot(w_ref[r0:r0 + 2 * ANGLES, 2 * ANGLES:], y_ref[high], preferred_element_type=jnp.float32)
                dest = high if h else low
                cosine = table_ref[level, 0, h]
                sinus = table_ref[level, 1, h]
                for tile in range(wide // LANES):
                    at = tile * LANES
                    zr = z[:ANGLES, at:at + LANES]
                    zi = z[ANGLES:, at:at + LANES]
                    re = zr * cosine - zi * sinus
                    im = zr * sinus + zi * cosine
                    if not last and (at < margin or at + LANES > given - margin):
                        inside = jnp.logical_and(cols + at >= 0, cols + at < total)
                        re = jnp.where(inside, re, 0.0)
                        im = jnp.where(inside, im, 0.0)
                    x_ref[dest, 0:ANGLES, at:at + LANES] = re.astype(jnp.bfloat16)
                    x_ref[dest, ANGLES:, at:at + LANES] = im.astype(jnp.bfloat16)
    for p in range(members):
        v = x_ref[p].astype(jnp.float32)
        out_ref[p] = pltpu.roll(v, wide - margin, 1)[:, :width].astype(jnp.bfloat16)


def merge_levels(start, taps, masks, weights, table, pieces, places, margin, total):
    members, rows, given = pieces.shape
    width = given - 2 * margin
    wide = -(-given // LANES) * LANES
    smem = pl.BlockSpec(memory_space=pltpu.SMEM)
    vmem = pl.BlockSpec(memory_space=pltpu.VMEM)
    return pl.pallas_call(
        functools.partial(merge_kernel, places=places, margin=margin, total=total),
        out_shape=jax.ShapeDtypeStruct((members, rows, width), jnp.bfloat16),
        in_specs=[smem, smem, vmem, vmem, vmem, vmem],
        out_specs=vmem,
        scratch_shapes=[
            pltpu.VMEM((members, rows, wide), jnp.bfloat16),
            pltpu.VMEM((members, rows, wide), jnp.bfloat16),
            pltpu.VMEM((4 * ANGLES, 4 * ANGLES), jnp.bfloat16),
        ],
        compiler_params=pltpu.CompilerParams(vmem_limit_bytes=48 * 2**20),
        name="merge_levels",
    )(start, taps, masks, weights, table, pieces)


def with_halo(cells, axis, margin):
    count = lax.axis_size(axis)
    head = cells[..., :margin]
    tail = cells[..., cells.shape[-1] - margin:]
    left = lax.ppermute(tail, axis, [(i, i + 1) for i in range(count - 1)])
    right = lax.ppermute(head, axis, [(i + 1, i) for i in range(count - 1)])
    return jnp.concatenate([left, cells, right], axis=-1)


def on_device(image, interp_weights, range_taps, range_shifts):
    _, groups, _, range_width = image.shape
    sub_count = lax.axis_size("sub")
    total = range_width * lax.axis_size("rng")
    sub_index = lax.axis_index("sub")
    masks = shift_masks(range_shifts)
    current = image
    for levels, bits, distinct in phases_of(sub_count.bit_length() - 1):
        members = 2 ** len(distinct)
        parts = members // groups
        width = range_width // parts
        margin = len(levels) * RIM
        first, end = levels[0], levels[-1] + 1
        spread = [sum(((p >> j) & 1) << bit for j, bit in enumerate(distinct)) for p in range(members)]
        bases = [i for i in range(sub_count) if all(not (i >> bit) & 1 for bit in distinct)]
        index_groups = None if len(bases) == 1 else [[base + s for s in spread] for base in bases]
        member = sum(((sub_index >> bit) & 1) << j for j, bit in enumerate(distinct))
        start = lax.axis_index("rng") * range_width + member // groups * width - margin
        padded = with_halo(current, "rng", margin)
        pieces = jnp.stack([
            padded[:, p % groups, :, p // groups * width:p // groups * width + width + 2 * margin]
            for p in range(members)
        ]).reshape(members, 2 * ANGLES, width + 2 * margin)
        pieces = lax.all_to_all(pieces, "sub", 0, 0, axis_index_groups=index_groups, tiled=True)
        merged = merge_levels(
            start.reshape(1).astype(jnp.int32), range_taps[first:end], masks[first:end],
            interp_weights[first:end], jnp.asarray(phase_table(levels, margin)), pieces,
            [distinct.index(bit) for bit in bits], margin, total)
        back = lax.all_to_all(merged, "sub", 0, 0, axis_index_groups=index_groups, tiled=True)
        back = back.reshape(parts, groups, 2, ANGLES, width)
        current = jnp.transpose(back, (2, 1, 3, 0, 4)).reshape(image.shape)
    return current


def solution(mesh):
    return jax.shard_map(
        on_device,
        mesh=mesh,
        in_specs=(P(None, ("img", "sub"), None, "rng"), P(), P(), P()),
        out_specs=P(None, ("img", "sub"), None, "rng"),
        check_vma=False,
    )
```

```python
import functools
import math

import jax
import jax.numpy as jnp
import numpy as np
from jax import lax
from jax.experimental import pallas as pl
from jax.experimental.pallas import tpu as pltpu
from jax.sharding import PartitionSpec as P

ANGLES = 128
RIM = 8
TAPS = 4
LEVELS = 4
LANES = 128
PERIOD = 64
ROWS = 32
CHUNKS = 2


def phases_of(bit_count):
    runs = []
    for level in range(LEVELS):
        bit = level % bit_count
        if runs and len(set(runs[-1][1] + [bit])) <= 2:
            runs[-1][0].append(level)
            runs[-1][1].append(bit)
        else:
            runs.append(([level], [bit]))
    return [(levels, bits, sorted(set(bits))) for levels, bits in runs]


def phase_table(levels, margin):
    cols = np.arange(LANES, dtype=np.int64) - margin
    rows = np.arange(2 * ANGLES, dtype=np.int64) + 1
    out = []
    for level in levels:
        wrapped = (cols[None, :] * rows[:, None] * (7 + level)) % PERIOD
        phase = wrapped.astype(np.float64) * (2.0 * math.pi / PERIOD)
        out.append(np.stack([np.cos(phase), np.sin(phase)]).reshape(2, 2, ANGLES, LANES))
    return np.stack(out).astype(np.float32)


def shift_masks(range_shifts):
    steps = range_shifts + RIM
    bits = [(steps >> k) & 1 for k in range(3)] + [1 - ((steps >> 3) & 1)]
    return jnp.stack(bits, axis=-1)


def merge_kernel(info_ref, taps_ref, masks_ref, weights_ref, table_ref, *refs, places, margin, total, members):
    in_refs, out_refs = refs[:members], refs[members:2 * members]
    x_ref, y_ref, w_ref = refs[2 * members:]
    _, _, wide = x_ref.shape
    given = in_refs[0].shape[-1]
    width = out_refs[0].shape[-1]
    start = info_ref[0]
    n_levels = len(places)
    x_ref[:, :, wide - LANES:] = jnp.zeros((members, 2 * ANGLES, LANES), jnp.bfloat16)
    for q in range(members):
        x_ref[q, :, 0:given] = in_refs[q][...]
    for level in range(n_levels):
        place = places[level]
        mine = (info_ref[1] >> place) & 1
        for h in range(2):
            for e in range(2):
                real = weights_ref[level, mine ^ e, mine ^ h, 0]
                imag = weights_ref[level, mine ^ e, mine ^ h, 1]
                r0, c0 = h * 2 * ANGLES, e * 2 * ANGLES
                w_ref[r0:r0 + ANGLES, c0:c0 + ANGLES] = real
                w_ref[r0:r0 + ANGLES, c0 + ANGLES:c0 + 2 * ANGLES] = -imag
                w_ref[r0 + ANGLES:r0 + 2 * ANGLES, c0:c0 + ANGLES] = imag
                w_ref[r0 + ANGLES:r0 + 2 * ANGLES, c0 + ANGLES:c0 + 2 * ANGLES] = real
        taps = [taps_ref[level, t] for t in range(TAPS)]

        for side in range(2):
            own = [p for p in range(members) if (p >> place) % 2 == side]

            def rows_step(block, carry, side=side, own=own, level=level, taps=taps, mine=mine):
                flags = masks_ref[level, mine ^ side, pl.ds(pl.multiple_of(block * ROWS, ROWS), ROWS), :]
                masks = [jnp.broadcast_to(flags[:, k:k + 1], (ROWS, wide)) != 0 for k in range(4)]
                for p in own:
                    for c in range(2):
                        rows = pl.ds(pl.multiple_of(c * ANGLES + block * ROWS, ROWS), ROWS)
                        cells = x_ref[p, rows, :].astype(jnp.float32)
                        after = pltpu.roll(cells, wide - 1, 1)
                        first = taps[0] * cells + taps[1] * after
                        second = taps[2] * cells + taps[3] * after
                        v = first + pltpu.roll(second, wide - 2, 1)
                        for k, by in ((0, wide - 1), (1, wide - 2), (2, wide - 4), (3, RIM)):
                            v = jnp.where(masks[k], pltpu.roll(v, by, 1), v)
                        y_ref[p, rows, :] = v.astype(jnp.bfloat16)
                return carry

            lax.fori_loop(0, ANGLES // ROWS, rows_step, 0)

        last = level == n_levels - 1
        cols = start + lax.broadcasted_iota(jnp.int32, (ANGLES, LANES), 1)
        for low in [p for p in range(members) if (p >> place) % 2 == 0]:
            high = low + 2 ** place
            for h in range(2):
                r0 = h * 2 * ANGLES
                z = jnp.dot(w_ref[r0:r0 + 2 * ANGLES, 0:2 * ANGLES], y_ref[low], preferred_element_type=jnp.float32)
                z = z + jnp.dot(w_ref[r0:r0 + 2 * ANGLES, 2 * ANGLES:], y_ref[high], preferred_element_type=jnp.float32)
                dest = high if h else low
                cosine = table_ref[level, 0, mine ^ h]
                sinus = table_ref[level, 1, mine ^ h]
                for tile in range(wide // LANES):
                    at = tile * LANES
                    zr = z[:ANGLES, at:at + LANES]
                    zi = z[ANGLES:, at:at + LANES]
                    re = zr * cosine - zi * sinus
                    im = zr * sinus + zi * cosine
                    if not last and (at < margin or at + LANES > given - margin):
                        inside = jnp.logical_and(cols + at >= 0, cols + at < total)
                        re = jnp.where(inside, re, 0.0)
                        im = jnp.where(inside, im, 0.0)
                    x_ref[dest, 0:ANGLES, at:at + LANES] = re.astype(jnp.bfloat16)
                    x_ref[dest, ANGLES:, at:at + LANES] = im.astype(jnp.bfloat16)
    for p in range(members):
        v = x_ref[p].astype(jnp.float32)
        out_refs[p][...] = pltpu.roll(v, wide - margin, 1)[:, :width].astype(jnp.bfloat16)


def merge_levels(info, taps, masks, weights, table, pieces, places, margin, total):
    members = len(pieces)
    rows, given = pieces[0].shape
    width = given - 2 * margin
    wide = -(-given // LANES) * LANES
    smem = pl.BlockSpec(memory_space=pltpu.SMEM)
    vmem = pl.BlockSpec(memory_space=pltpu.VMEM)
    return pl.pallas_call(
        functools.partial(merge_kernel, places=places, margin=margin, total=total, members=members),
        out_shape=[jax.ShapeDtypeStruct((rows, width), jnp.bfloat16)] * members,
        in_specs=[smem, smem] + [vmem] * (3 + members),
        out_specs=[vmem] * members,
        scratch_shapes=[
            pltpu.VMEM((members, rows, wide), jnp.bfloat16),
            pltpu.VMEM((members, rows, wide), jnp.bfloat16),
            pltpu.VMEM((4 * ANGLES, 4 * ANGLES), jnp.bfloat16),
        ],
        compiler_params=pltpu.CompilerParams(vmem_limit_bytes=32 * 2**20),
        name="merge_levels",
    )(info, taps, masks, weights, table, *pieces)


def with_halo(cells, axis, margin):
    count = lax.axis_size(axis)
    head = cells[..., :margin]
    tail = cells[..., cells.shape[-1] - margin:]
    left = lax.ppermute(tail, axis, [(i, i + 1) for i in range(count - 1)])
    right = lax.ppermute(head, axis, [(i + 1, i) for i in range(count - 1)])
    return jnp.concatenate([left, cells, right], axis=-1)


def pick(items, q, member):
    def chosen(j, slot):
        if j < 0:
            return items[slot]
        return jnp.where((member >> j) & 1 == 1, chosen(j - 1, slot ^ (1 << j)), chosen(j - 1, slot))
    return chosen(len(items).bit_length() - 2, q)


def swap(value, q, distinct, sub_count):
    if q == 0:
        return value
    mask = sum(((q >> j) & 1) << bit for j, bit in enumerate(distinct))
    return lax.ppermute(value, "sub", [(i, i ^ mask) for i in range(sub_count)])


def on_device(image, interp_weights, range_taps, range_shifts):
    _, groups, _, range_width = image.shape
    sub_count = lax.axis_size("sub")
    total = range_width * lax.axis_size("rng")
    sub_index = lax.axis_index("sub")
    masks = shift_masks(range_shifts)
    current = image
    for levels, bits, distinct in phases_of(sub_count.bit_length() - 1):
        members = 2 ** len(distinct)
        parts = members // groups
        width = range_width // parts
        step = width // CHUNKS
        margin = len(levels) * RIM
        first, end = levels[0], levels[-1] + 1
        member = sum(((sub_index >> bit) & 1) << j for j, bit in enumerate(distinct))
        start = lax.axis_index("rng") * range_width + (member >> (groups.bit_length() - 1)) * width - margin
        padded = with_halo(current, "rng", margin)
        table = jnp.asarray(phase_table(levels, margin))
        columns = [[None] * CHUNKS for _ in range(members)]
        pieces = []
        for chunk in range(CHUNKS):
            windows = []
            for p in range(members):
                at = p // groups * width + chunk * step
                windows.append(padded[:, p % groups, :, at:at + step + 2 * margin])
            pieces.append([
                swap(pick(windows, q, member).reshape(2 * ANGLES, step + 2 * margin), q, distinct, sub_count)
                for q in range(members)
            ])
        for chunk in range(CHUNKS):
            info = jnp.stack([start + chunk * step, member]).astype(jnp.int32)
            merged = merge_levels(
                info, range_taps[first:end], masks[first:end], interp_weights[first:end], table,
                pieces[chunk], [distinct.index(bit) for bit in bits], margin, total)
            back = [swap(merged[q], q, distinct, sub_count) for q in range(members)]
            for p in range(members):
                columns[p][chunk] = pick(back, p, member).reshape(2, ANGLES, step)
        current = jnp.stack([
            jnp.concatenate([columns[part * groups + m][chunk] for part in range(parts) for chunk in range(CHUNKS)], axis=-1)
            for m in range(groups)
        ], axis=1)
    return current


def solution(mesh):
    return jax.shard_map(
        on_device,
        mesh=mesh,
        in_specs=(P(None, ("img", "sub"), None, "rng"), P(), P(), P()),
        out_specs=P(None, ("img", "sub"), None, "rng"),
        check_vma=False,
    )
```

```python
import functools
import math

import jax
import jax.numpy as jnp
import numpy as np
from jax import lax
from jax.experimental import pallas as pl
from jax.experimental.pallas import tpu as pltpu
from jax.sharding import PartitionSpec as P

ANGLES = 128
RIM = 8
TAPS = 4
LEVELS = 4
LANES = 128
PERIOD = 64
ROWS = 32
CHUNKS = 1


def phases_of(bit_count):
    runs = []
    for level in range(LEVELS):
        bit = level % bit_count
        if runs and len(set(runs[-1][1] + [bit])) <= 2:
            runs[-1][0].append(level)
            runs[-1][1].append(bit)
        else:
            runs.append(([level], [bit]))
    return [(levels, bits, sorted(set(bits))) for levels, bits in runs]


def phase_table(levels, margin):
    cols = np.arange(LANES, dtype=np.int64) - margin
    rows = np.arange(2 * ANGLES, dtype=np.int64) + 1
    out = []
    for level in levels:
        wrapped = (cols[None, :] * rows[:, None] * (7 + level)) % PERIOD
        phase = wrapped.astype(np.float64) * (2.0 * math.pi / PERIOD)
        out.append(np.stack([np.cos(phase), np.sin(phase)]).reshape(2, 2, ANGLES, LANES))
    return np.stack(out).astype(np.float32)


def shift_masks(range_shifts):
    steps = range_shifts + RIM
    bits = [(steps >> k) & 1 for k in range(3)] + [1 - ((steps >> 3) & 1)]
    return jnp.stack(bits, axis=-1).astype(jnp.float32)


def merge_kernel(info_ref, taps_ref, masks_ref, weights_ref, table_ref, *refs, places, margin, total, members):
    in_refs, out_refs = refs[:members], refs[members:2 * members]
    x_ref, y_ref, w_ref = refs[2 * members:]
    _, _, wide = x_ref.shape
    given = in_refs[0].shape[-1]
    width = out_refs[0].shape[-1]
    start = info_ref[0]
    n_levels = len(places)
    x_ref[:, :, wide - LANES:] = jnp.zeros((members, 2 * ANGLES, LANES), jnp.bfloat16)
    for q in range(members):
        x_ref[q, :, 0:given] = in_refs[q][...]
    for level in range(n_levels):
        place = places[level]
        mine = (info_ref[1] >> place) & 1
        for h in range(2):
            for e in range(2):
                real = weights_ref[level, mine ^ e, mine ^ h, 0]
                imag = weights_ref[level, mine ^ e, mine ^ h, 1]
                r0, c0 = h * 2 * ANGLES, e * 2 * ANGLES
                w_ref[r0:r0 + ANGLES, c0:c0 + ANGLES] = real
                w_ref[r0:r0 + ANGLES, c0 + ANGLES:c0 + 2 * ANGLES] = -imag
                w_ref[r0 + ANGLES:r0 + 2 * ANGLES, c0:c0 + ANGLES] = imag
                w_ref[r0 + ANGLES:r0 + 2 * ANGLES, c0 + ANGLES:c0 + 2 * ANGLES] = real
        taps = [taps_ref[level, t] for t in range(TAPS)]

        for side in range(2):
            own = [p for p in range(members) if (p >> place) % 2 == side]

            def rows_step(block, carry, side=side, own=own, level=level, taps=taps, mine=mine):
                flags = masks_ref[level, mine ^ side, pl.ds(pl.multiple_of(block * ROWS, ROWS), ROWS), :]
                masks = [jnp.broadcast_to(flags[:, k:k + 1], (ROWS, wide)).astype(jnp.bfloat16) > 0 for k in range(4)]
                for p in own:
                    for c in range(2):
                        rows = pl.ds(pl.multiple_of(c * ANGLES + block * ROWS, ROWS), ROWS)
                        cells = x_ref[p, rows, :].astype(jnp.float32)
                        after = pltpu.roll(cells, wide - 1, 1)
                        first = taps[0] * cells + taps[1] * after
                        second = taps[2] * cells + taps[3] * after
                        v = (first + pltpu.roll(second, wide - 2, 1)).astype(jnp.bfloat16)
                        for k, by in ((0, wide - 1), (1, wide - 2), (2, wide - 4), (3, RIM)):
                            v = jnp.where(masks[k], pltpu.roll(v, by, 1), v)
                        pair = p % 2 ** place + p // 2 ** (place + 1) * 2 ** place
                        spot = pl.ds(pl.multiple_of((2 * side + c) * ANGLES + block * ROWS, ROWS), ROWS)
                        y_ref[pair, spot, :] = v
                return carry

            lax.fori_loop(0, ANGLES // ROWS, rows_step, 0)

        last = level == n_levels - 1
        cols = start + lax.broadcasted_iota(jnp.int32, (ANGLES, LANES), 1)
        for low in [p for p in range(members) if (p >> place) % 2 == 0]:
            high = low + 2 ** place
            for h in range(2):
                r0 = h * 2 * ANGLES
                pair = low % 2 ** place + low // 2 ** (place + 1) * 2 ** place
                z = jnp.dot(w_ref[r0:r0 + 2 * ANGLES, :], y_ref[pair], preferred_element_type=jnp.float32)
                dest = high if h else low
                cosine = table_ref[level, 0, mine ^ h]
                sinus = table_ref[level, 1, mine ^ h]
                for tile in range(wide // LANES):
                    at = tile * LANES
                    zr = z[:ANGLES, at:at + LANES]
                    zi = z[ANGLES:, at:at + LANES]
                    re = zr * cosine - zi * sinus
                    im = zr * sinus + zi * cosine
                    if not last and (at < margin or at + LANES > given - margin):
                        inside = jnp.logical_and(cols + at >= 0, cols + at < total)
                        re = jnp.where(inside, re, 0.0)
                        im = jnp.where(inside, im, 0.0)
                    x_ref[dest, 0:ANGLES, at:at + LANES] = re.astype(jnp.bfloat16)
                    x_ref[dest, ANGLES:, at:at + LANES] = im.astype(jnp.bfloat16)
    for p in range(members):
        v = x_ref[p]
        out_refs[p][...] = pltpu.roll(v, wide - margin, 1)[:, :width]


def merge_levels(info, taps, masks, weights, table, pieces, places, margin, total):
    members = len(pieces)
    rows, given = pieces[0].shape
    width = given - 2 * margin
    wide = -(-given // LANES) * LANES
    smem = pl.BlockSpec(memory_space=pltpu.SMEM)
    vmem = pl.BlockSpec(memory_space=pltpu.VMEM)
    return pl.pallas_call(
        functools.partial(merge_kernel, places=places, margin=margin, total=total, members=members),
        out_shape=[jax.ShapeDtypeStruct((rows, width), jnp.bfloat16)] * members,
        in_specs=[smem, smem] + [vmem] * (3 + members),
        out_specs=[vmem] * members,
        scratch_shapes=[
            pltpu.VMEM((members, rows, wide), jnp.bfloat16),
            pltpu.VMEM((members // 2, 2 * rows, wide), jnp.bfloat16),
            pltpu.VMEM((4 * ANGLES, 4 * ANGLES), jnp.bfloat16),
        ],
        compiler_params=pltpu.CompilerParams(vmem_limit_bytes=32 * 2**20),
        name="merge_levels",
    )(info, taps, masks, weights, table, *pieces)


def with_halo(cells, axis, margin):
    count = lax.axis_size(axis)
    head = cells[..., :margin]
    tail = cells[..., cells.shape[-1] - margin:]
    left = lax.ppermute(tail, axis, [(i, i + 1) for i in range(count - 1)])
    right = lax.ppermute(head, axis, [(i + 1, i) for i in range(count - 1)])
    return jnp.concatenate([left, cells, right], axis=-1)


def pick(items, q, member):
    def chosen(j, slot):
        if j < 0:
            return items[slot]
        return jnp.where((member >> j) & 1 == 1, chosen(j - 1, slot ^ (1 << j)), chosen(j - 1, slot))
    return chosen(len(items).bit_length() - 2, q)


def swap(value, q, distinct, sub_count):
    if q == 0:
        return value
    mask = sum(((q >> j) & 1) << bit for j, bit in enumerate(distinct))
    return lax.ppermute(value, "sub", [(i, i ^ mask) for i in range(sub_count)])


def on_device(image, interp_weights, range_taps, range_shifts):
    _, groups, _, range_width = image.shape
    sub_count = lax.axis_size("sub")
    total = range_width * lax.axis_size("rng")
    sub_index = lax.axis_index("sub")
    masks = shift_masks(range_shifts)
    current = image
    for levels, bits, distinct in phases_of(sub_count.bit_length() - 1):
        members = 2 ** len(distinct)
        parts = members // groups
        width = range_width // parts
        step = width // CHUNKS
        margin = len(levels) * RIM
        first, end = levels[0], levels[-1] + 1
        member = sum(((sub_index >> bit) & 1) << j for j, bit in enumerate(distinct))
        start = lax.axis_index("rng") * range_width + (member >> (groups.bit_length() - 1)) * width - margin
        padded = with_halo(current, "rng", margin)
        table = jnp.asarray(phase_table(levels, margin))
        columns = [[None] * CHUNKS for _ in range(members)]
        pieces = []
        for chunk in range(CHUNKS):
            windows = []
            for p in range(members):
                at = p // groups * width + chunk * step
                windows.append(padded[:, p % groups, :, at:at + step + 2 * margin])
            pieces.append([
                swap(pick(windows, q, member).reshape(2 * ANGLES, step + 2 * margin), q, distinct, sub_count)
                for q in range(members)
            ])
        for chunk in range(CHUNKS):
            info = jnp.stack([start + chunk * step, member]).astype(jnp.int32)
            merged = merge_levels(
                info, range_taps[first:end], masks[first:end], interp_weights[first:end], table,
                pieces[chunk], [distinct.index(bit) for bit in bits], margin, total)
            back = [swap(merged[q], q, distinct, sub_count) for q in range(members)]
            for p in range(members):
                columns[p][chunk] = pick(back, p, member).reshape(2, ANGLES, step)
        current = jnp.stack([
            jnp.concatenate([columns[part * groups + m][chunk] for part in range(parts) for chunk in range(CHUNKS)], axis=-1)
            for m in range(groups)
        ], axis=1)
    return current


def solution(mesh):
    return jax.shard_map(
        on_device,
        mesh=mesh,
        in_specs=(P(None, ("img", "sub"), None, "rng"), P(), P(), P()),
        out_specs=P(None, ("img", "sub"), None, "rng"),
        check_vma=False,
    )
```

```python
import functools
import math

import jax
import jax.numpy as jnp
import numpy as np
from jax import lax
from jax.experimental import pallas as pl
from jax.experimental.pallas import tpu as pltpu
from jax.sharding import PartitionSpec as P

ANGLES = 128
RIM = 8
TAPS = 4
LEVELS = 4
LANES = 128
PERIOD = 64
ROWS = 32


def phases_of(bit_count):
    runs = []
    for level in range(LEVELS):
        bit = level % bit_count
        if runs and len(set(runs[-1][1] + [bit])) <= 2:
            runs[-1][0].append(level)
            runs[-1][1].append(bit)
        else:
            runs.append(([level], [bit]))
    return [(levels, bits, sorted(set(bits))) for levels, bits in runs]


def phase_table(levels):
    cols = np.arange(LANES, dtype=np.int64)
    rows = np.arange(2 * ANGLES, dtype=np.int64) + 1
    out = []
    for level in levels:
        wrapped = (cols[None, :] * rows[:, None] * (7 + level)) % PERIOD
        phase = wrapped.astype(np.float64) * (2.0 * math.pi / PERIOD)
        out.append(np.stack([np.cos(phase), np.sin(phase)]).reshape(2, 2, ANGLES, LANES))
    return np.stack(out).astype(np.float32)


def shift_masks(range_shifts):
    steps = range_shifts + RIM
    bits = [(steps >> k) & 1 for k in range(3)] + [1 - ((steps >> 3) & 1)]
    return jnp.stack(bits, axis=-1).astype(jnp.float32)


def merge_kernel(info_ref, taps_ref, masks_ref, weights_ref, table_ref, *refs, places, margin, total, members):
    body_refs, strip_refs, out_refs = (refs[i * members:(i + 1) * members] for i in range(3))
    x_ref, y_ref, w_ref = refs[3 * members:]
    _, _, wide = x_ref.shape
    width = out_refs[0].shape[-1]
    start = info_ref[0]
    n_levels = len(places)
    first_part = info_ref[2] == 0
    gap = jnp.zeros((2 * ANGLES, wide - width - 2 * margin), jnp.float32)
    for q in range(members):
        x_ref[q, :, 0:width] = body_refs[q][:, 0:width]
        inner = body_refs[q][:, width:width + margin].astype(jnp.float32)
        outer = strip_refs[q][...].astype(jnp.float32)
        right = jnp.where(first_part, inner, outer)
        left = jnp.where(first_part, outer, inner)
        x_ref[q, :, width:] = jnp.concatenate([right, gap, left], axis=1).astype(jnp.bfloat16)
    for level in range(n_levels):
        place = places[level]
        mine = (info_ref[1] >> place) & 1
        for h in range(2):
            for e in range(2):
                real = weights_ref[level, mine ^ e, mine ^ h, 0]
                imag = weights_ref[level, mine ^ e, mine ^ h, 1]
                r0, c0 = h * 2 * ANGLES, e * 2 * ANGLES
                w_ref[r0:r0 + ANGLES, c0:c0 + ANGLES] = real
                w_ref[r0:r0 + ANGLES, c0 + ANGLES:c0 + 2 * ANGLES] = -imag
                w_ref[r0 + ANGLES:r0 + 2 * ANGLES, c0:c0 + ANGLES] = imag
                w_ref[r0 + ANGLES:r0 + 2 * ANGLES, c0 + ANGLES:c0 + 2 * ANGLES] = real
        taps = [taps_ref[level, t] for t in range(TAPS)]

        for side in range(2):
            own = [p for p in range(members) if (p >> place) % 2 == side]

            def rows_step(block, carry, side=side, own=own, level=level, taps=taps, mine=mine):
                flags = masks_ref[level, mine ^ side, pl.ds(pl.multiple_of(block * ROWS, ROWS), ROWS), :]
                masks = [jnp.broadcast_to(flags[:, k:k + 1], (ROWS, wide)).astype(jnp.bfloat16) > 0 for k in range(4)]
                for p in own:
                    for c in range(2):
                        rows = pl.ds(pl.multiple_of(c * ANGLES + block * ROWS, ROWS), ROWS)
                        cells = x_ref[p, rows, :].astype(jnp.float32)
                        after = pltpu.roll(cells, wide - 1, 1)
                        first = taps[0] * cells + taps[1] * after
                        second = taps[2] * cells + taps[3] * after
                        v = (first + pltpu.roll(second, wide - 2, 1)).astype(jnp.bfloat16)
                        for k, by in ((0, wide - 1), (1, wide - 2), (2, wide - 4), (3, RIM)):
                            v = jnp.where(masks[k], pltpu.roll(v, by, 1), v)
                        pair = p % 2 ** place + p // 2 ** (place + 1) * 2 ** place
                        spot = pl.ds(pl.multiple_of((2 * side + c) * ANGLES + block * ROWS, ROWS), ROWS)
                        y_ref[pair, spot, :] = v
                return carry

            lax.fori_loop(0, ANGLES // ROWS, rows_step, 0)

        last = level == n_levels - 1
        lane = lax.broadcasted_iota(jnp.int32, (ANGLES, LANES), 1)
        cols = start + jnp.where(lane < LANES // 2, lane + width, lane - LANES)
        for low in [p for p in range(members) if (p >> place) % 2 == 0]:
            high = low + 2 ** place
            for h in range(2):
                r0 = h * 2 * ANGLES
                pair = low % 2 ** place + low // 2 ** (place + 1) * 2 ** place
                z = jnp.dot(w_ref[r0:r0 + 2 * ANGLES, :], y_ref[pair], preferred_element_type=jnp.float32)
                dest = high if h else low
                cosine = table_ref[level, 0, mine ^ h]
                sinus = table_ref[level, 1, mine ^ h]
                for tile in range((width if last else wide) // LANES):
                    at = tile * LANES
                    zr = z[:ANGLES, at:at + LANES]
                    zi = z[ANGLES:, at:at + LANES]
                    re = zr * cosine - zi * sinus
                    im = zr * sinus + zi * cosine
                    if at == width:
                        inside = jnp.logical_and(cols >= 0, cols < total)
                        re = jnp.where(inside, re, 0.0)
                        im = jnp.where(inside, im, 0.0)
                    x_ref[dest, 0:ANGLES, at:at + LANES] = re.astype(jnp.bfloat16)
                    x_ref[dest, ANGLES:, at:at + LANES] = im.astype(jnp.bfloat16)
    for p in range(members):
        out_refs[p][...] = x_ref[p, :, 0:width]


def merge_levels(info, taps, masks, weights, table, bodies, strips, places, margin, total):
    members = len(bodies)
    rows, given = bodies[0].shape
    width = given - margin
    wide = width + LANES
    smem = pl.BlockSpec(memory_space=pltpu.SMEM)
    vmem = pl.BlockSpec(memory_space=pltpu.VMEM)
    return pl.pallas_call(
        functools.partial(merge_kernel, places=places, margin=margin, total=total, members=members),
        out_shape=[jax.ShapeDtypeStruct((rows, width), jnp.bfloat16)] * members,
        in_specs=[smem, smem] + [vmem] * (3 + 2 * members),
        out_specs=[vmem] * members,
        scratch_shapes=[
            pltpu.VMEM((members, rows, wide), jnp.bfloat16),
            pltpu.VMEM((members // 2, 2 * rows, wide), jnp.bfloat16),
            pltpu.VMEM((4 * ANGLES, 4 * ANGLES), jnp.bfloat16),
        ],
        compiler_params=pltpu.CompilerParams(vmem_limit_bytes=32 * 2**20),
        name="merge_levels",
    )(info, taps, masks, weights, table, *bodies, *strips)


def pick(items, q, member):
    def chosen(j, slot):
        if j < 0:
            return items[slot]
        return jnp.where((member >> j) & 1 == 1, chosen(j - 1, slot ^ (1 << j)), chosen(j - 1, slot))
    return chosen(len(items).bit_length() - 2, q)


def swap(value, q, distinct, sub_count):
    if q == 0:
        return value
    mask = sum(((q >> j) & 1) << bit for j, bit in enumerate(distinct))
    return lax.ppermute(value, "sub", [(i, i ^ mask) for i in range(sub_count)])


def swap_strip(value, q, distinct, groups, sub_count):
    mask = sum(((q >> j) & 1) << bit for j, bit in enumerate(distinct))
    count = lax.axis_size("rng")
    pairs = []
    for source in range(sub_count):
        dest = source ^ mask
        member = sum(((dest >> bit) & 1) << j for j, bit in enumerate(distinct))
        move = 1 if member // groups == 0 else -1
        pairs += [(source * count + i, dest * count + i + move) for i in range(count) if 0 <= i + move < count]
    return lax.ppermute(value, ("sub", "rng"), pairs)


def on_device(image, interp_weights, range_taps, range_shifts):
    _, groups, _, range_width = image.shape
    sub_count = lax.axis_size("sub")
    total = range_width * lax.axis_size("rng")
    sub_index = lax.axis_index("sub")
    masks = shift_masks(range_shifts)
    current = image
    for levels, bits, distinct in phases_of(sub_count.bit_length() - 1):
        members = 2 ** len(distinct)
        parts = members // groups
        width = range_width // parts
        margin = len(levels) * RIM
        assert parts == 2 and width % LANES == 0 and 2 * margin < LANES
        first, end = levels[0], levels[-1] + 1
        member = sum(((sub_index >> bit) & 1) << j for j, bit in enumerate(distinct))
        part = member >> (groups.bit_length() - 1)
        start = lax.axis_index("rng") * range_width + part * width
        bodies, strips = [], []
        for p in range(members):
            rows = current[:, p % groups].reshape(2 * ANGLES, range_width)
            if p // groups == 0:
                bodies.append(rows[:, :width + margin])
                strips.append(rows[:, range_width - margin:])
            else:
                bodies.append(jnp.concatenate([rows[:, width:], rows[:, width - margin:width]], axis=1))
                strips.append(rows[:, :margin])
        bodies = [swap(pick(bodies, q, member), q, distinct, sub_count) for q in range(members)]
        strips = [swap_strip(pick(strips, q, member), q, distinct, groups, sub_count) for q in range(members)]
        info = jnp.stack([start, member, part]).astype(jnp.int32)
        merged = merge_levels(
            info, range_taps[first:end], masks[first:end], interp_weights[first:end], jnp.asarray(phase_table(levels)),
            bodies, strips, [distinct.index(bit) for bit in bits], margin, total)
        back = [swap(merged[q], q, distinct, sub_count) for q in range(members)]
        columns = [pick(back, p, member).reshape(2, ANGLES, width) for p in range(members)]
        current = jnp.stack([
            jnp.concatenate([columns[k * groups + m] for k in range(parts)], axis=-1) for m in range(groups)
        ], axis=1)
    return current


def solution(mesh):
    return jax.shard_map(
        on_device,
        mesh=mesh,
        in_specs=(P(None, ("img", "sub"), None, "rng"), P(), P(), P()),
        out_specs=P(None, ("img", "sub"), None, "rng"),
        check_vma=False,
    )
```

```python
import functools
import math

import jax
import jax.numpy as jnp
import numpy as np
from jax import lax
from jax.experimental import pallas as pl
from jax.experimental.pallas import tpu as pltpu
from jax.sharding import PartitionSpec as P

ANGLES = 128
RIM = 8
TAPS = 4
LEVELS = 4
LANES = 128
PERIOD = 64
ROWS = 32


def phases_of(bit_count):
    runs = []
    for level in range(LEVELS):
        bit = level % bit_count
        if runs and len(set(runs[-1][1] + [bit])) <= 2:
            runs[-1][0].append(level)
            runs[-1][1].append(bit)
        else:
            runs.append(([level], [bit]))
    return [(levels, bits, sorted(set(bits))) for levels, bits in runs]


def phase_table(levels):
    cols = np.arange(LANES, dtype=np.int64)
    rows = np.arange(2 * ANGLES, dtype=np.int64) + 1
    out = []
    for level in levels:
        wrapped = (cols[None, :] * rows[:, None] * (7 + level)) % PERIOD
        phase = wrapped.astype(np.float64) * (2.0 * math.pi / PERIOD)
        out.append(np.stack([np.cos(phase), np.sin(phase)]).reshape(2, 2, ANGLES, LANES))
    return np.stack(out).astype(np.float32)


def shift_masks(range_shifts):
    steps = range_shifts + RIM
    bits = [(steps >> k) & 1 for k in range(3)] + [1 - ((steps >> 3) & 1)]
    return jnp.stack(bits, axis=-1).astype(jnp.float32)


def merge_kernel(info_ref, taps_ref, masks_ref, weights_ref, table_ref, *refs, places, margin, total, members):
    body_refs, strip_refs, out_refs = (refs[i * members:(i + 1) * members] for i in range(3))
    x_ref, y_ref, w_ref = refs[3 * members:]
    _, _, wide = x_ref.shape
    width = out_refs[0].shape[-1]
    start = info_ref[0]
    n_levels = len(places)
    first_part = info_ref[2] == 0
    gap = jnp.zeros((2 * ANGLES, wide - width - 2 * margin), jnp.float32)
    for q in range(members):
        x_ref[q, :, 0:width] = body_refs[q][:, 0:width]
        inner = body_refs[q][:, width:width + margin].astype(jnp.float32)
        outer = strip_refs[q][...].astype(jnp.float32)
        right = jnp.where(first_part, inner, outer)
        left = jnp.where(first_part, outer, inner)
        x_ref[q, :, width:] = jnp.concatenate([right, gap, left], axis=1).astype(jnp.bfloat16)
    for level in range(n_levels):
        place = places[level]
        mine = (info_ref[1] >> place) & 1
        for h in range(2):
            for e in range(2):
                real = weights_ref[level, mine ^ e, mine ^ h, 0]
                imag = weights_ref[level, mine ^ e, mine ^ h, 1]
                r0, c0 = h * 2 * ANGLES, e * 2 * ANGLES
                w_ref[r0:r0 + ANGLES, c0:c0 + ANGLES] = real
                w_ref[r0:r0 + ANGLES, c0 + ANGLES:c0 + 2 * ANGLES] = -imag
                w_ref[r0 + ANGLES:r0 + 2 * ANGLES, c0:c0 + ANGLES] = imag
                w_ref[r0 + ANGLES:r0 + 2 * ANGLES, c0 + ANGLES:c0 + 2 * ANGLES] = real
        taps = [taps_ref[level, t] for t in range(TAPS)]

        for side in range(2):
            own = [p for p in range(members) if (p >> place) % 2 == side]

            def rows_step(block, carry, side=side, own=own, level=level, taps=taps, mine=mine):
                flags = masks_ref[level, mine ^ side, pl.ds(pl.multiple_of(block * ROWS, ROWS), ROWS), :]
                masks = [jnp.broadcast_to(flags[:, k:k + 1], (ROWS, wide)).astype(jnp.bfloat16) > 0 for k in range(4)]
                for p in own:
                    for c in range(2):
                        rows = pl.ds(pl.multiple_of(c * ANGLES + block * ROWS, ROWS), ROWS)
                        cells = x_ref[p, rows, :].astype(jnp.float32)
                        after = pltpu.roll(cells, wide - 1, 1)
                        first = taps[0] * cells + taps[1] * after
                        second = taps[2] * cells + taps[3] * after
                        v = (first + pltpu.roll(second, wide - 2, 1)).astype(jnp.bfloat16)
                        for k, by in ((0, wide - 1), (1, wide - 2), (2, wide - 4), (3, RIM)):
                            v = jnp.where(masks[k], pltpu.roll(v, by, 1), v)
                        pair = p % 2 ** place + p // 2 ** (place + 1) * 2 ** place
                        spot = pl.ds(pl.multiple_of((2 * side + c) * ANGLES + block * ROWS, ROWS), ROWS)
                        y_ref[pair, spot, :] = v
                return carry

            lax.fori_loop(0, ANGLES // ROWS, rows_step, 0)

        last = level == n_levels - 1
        lane = lax.broadcasted_iota(jnp.int32, (ANGLES, LANES), 1)
        cols = start + jnp.where(lane < LANES // 2, lane + width, lane - LANES)
        for low in [p for p in range(members) if (p >> place) % 2 == 0]:
            high = low + 2 ** place
            for h in range(2):
                r0 = h * 2 * ANGLES
                pair = low % 2 ** place + low // 2 ** (place + 1) * 2 ** place
                z = jnp.dot(w_ref[r0:r0 + 2 * ANGLES, :], y_ref[pair], preferred_element_type=jnp.float32)
                dest = high if h else low
                cosine = table_ref[level, 0, mine ^ h]
                sinus = table_ref[level, 1, mine ^ h]
                for tile in range((width if last else wide) // LANES):
                    at = tile * LANES
                    zr = z[:ANGLES, at:at + LANES]
                    zi = z[ANGLES:, at:at + LANES]
                    re = zr * cosine - zi * sinus
                    im = zr * sinus + zi * cosine
                    if at == width:
                        inside = jnp.logical_and(cols >= 0, cols < total)
                        re = jnp.where(inside, re, 0.0)
                        im = jnp.where(inside, im, 0.0)
                    x_ref[dest, 0:ANGLES, at:at + LANES] = re.astype(jnp.bfloat16)
                    x_ref[dest, ANGLES:, at:at + LANES] = im.astype(jnp.bfloat16)
    for p in range(members):
        out_refs[p][...] = x_ref[p, :, 0:width]


def merge_levels(info, taps, masks, weights, table, bodies, strips, places, margin, total):
    members = len(bodies)
    rows, given = bodies[0].shape
    width = given - margin
    wide = width + LANES
    smem = pl.BlockSpec(memory_space=pltpu.SMEM)
    vmem = pl.BlockSpec(memory_space=pltpu.VMEM)
    return pl.pallas_call(
        functools.partial(merge_kernel, places=places, margin=margin, total=total, members=members),
        out_shape=[jax.ShapeDtypeStruct((rows, width), jnp.bfloat16)] * members,
        in_specs=[smem, smem] + [vmem] * (3 + 2 * members),
        out_specs=[vmem] * members,
        scratch_shapes=[
            pltpu.VMEM((members, rows, wide), jnp.bfloat16),
            pltpu.VMEM((members // 2, 2 * rows, wide), jnp.bfloat16),
            pltpu.VMEM((4 * ANGLES, 4 * ANGLES), jnp.bfloat16),
        ],
        compiler_params=pltpu.CompilerParams(vmem_limit_bytes=32 * 2**20),
        name="merge_levels",
    )(info, taps, masks, weights, table, *bodies, *strips)


def pick(items, q, member):
    def chosen(j, slot):
        if j < 0:
            return items[slot]
        return jnp.where((member >> j) & 1 == 1, chosen(j - 1, slot ^ (1 << j)), chosen(j - 1, slot))
    return chosen(len(items).bit_length() - 2, q)


def swap(value, q, distinct, sub_count):
    if q == 0:
        return value
    mask = sum(((q >> j) & 1) << bit for j, bit in enumerate(distinct))
    return lax.ppermute(value, "sub", [(i, i ^ mask) for i in range(sub_count)])


def swap_strip(value, q, distinct, groups, sub_count):
    mask = sum(((q >> j) & 1) << bit for j, bit in enumerate(distinct))
    count = lax.axis_size("rng")
    pairs = []
    for source in range(sub_count):
        dest = source ^ mask
        member = sum(((dest >> bit) & 1) << j for j, bit in enumerate(distinct))
        move = 1 if member // groups == 0 else -1
        pairs += [(source * count + i, dest * count + i + move) for i in range(count) if 0 <= i + move < count]
    return lax.ppermute(value, ("sub", "rng"), pairs)


def on_device(image, interp_weights, range_taps, range_shifts):
    _, groups, _, range_width = image.shape
    sub_count = lax.axis_size("sub")
    total = range_width * lax.axis_size("rng")
    sub_index = lax.axis_index("sub")
    masks = shift_masks(range_shifts)
    current = image
    for levels, bits, distinct in phases_of(sub_count.bit_length() - 1):
        members = 2 ** len(distinct)
        parts = members // groups
        width = range_width // parts
        margin = len(levels) * RIM
        assert parts == 2 and width % LANES == 0 and 2 * margin < LANES
        first, end = levels[0], levels[-1] + 1
        member = sum(((sub_index >> bit) & 1) << j for j, bit in enumerate(distinct))
        part = member >> (groups.bit_length() - 1)
        start = lax.axis_index("rng") * range_width + part * width
        bodies, strips = [], []
        for p in range(members):
            rows = current[:, p % groups].reshape(2 * ANGLES, range_width)
            if p // groups == 0:
                bodies.append(rows[:, :width + margin])
                strips.append(rows[:, range_width - margin:])
            else:
                bodies.append(jnp.concatenate([rows[:, width:], rows[:, width - margin:width]], axis=1))
                strips.append(rows[:, :margin])
        bodies = [swap(pick(bodies, q, member), q, distinct, sub_count) for q in range(members)]
        strips, bodies[1] = lax.optimization_barrier(([pick(strips, q, member) for q in range(members)], bodies[1]))
        strips = [swap_strip(strips[q], q, distinct, groups, sub_count) for q in range(members)]
        info = jnp.stack([start, member, part]).astype(jnp.int32)
        merged = merge_levels(
            info, range_taps[first:end], masks[first:end], interp_weights[first:end], jnp.asarray(phase_table(levels)),
            bodies, strips, [distinct.index(bit) for bit in bits], margin, total)
        back = [swap(merged[q], q, distinct, sub_count) for q in range(members)]
        columns = [pick(back, p, member).reshape(2, ANGLES, width) for p in range(members)]
        current = jnp.stack([
            jnp.concatenate([columns[k * groups + m] for k in range(parts)], axis=-1) for m in range(groups)
        ], axis=1)
    return current


def solution(mesh):
    return jax.shard_map(
        on_device,
        mesh=mesh,
        in_specs=(P(None, ("img", "sub"), None, "rng"), P(), P(), P()),
        out_specs=P(None, ("img", "sub"), None, "rng"),
        check_vma=False,
    )
```
